128 devices in a mesh: req: 32 (over z, x, core), tp: 4 (over y).
Axes of the slice: x: 4, y: 4, z: 4, core: 2. Of those that a mesh axis runs over, the one named last changes fastest.
Arguments:
- tokens: bfloat16 [12288, 5120], P('req'), may hold values from -40 to 40
- w_query: bfloat16 [5120, 2560], P(None, 'tp'), may hold values from -0.125 to 0.125
- query_bias: float32 [2560], P('tp'), may hold values from -24 to 24
- w_keyval: bfloat16 [5120, 1024], P(None, 'tp'), may hold values from -0.21875 to 0.21875
- keyval_bias: float32 [1024], P('tp'), may hold values from -2.5 to 2.5
- w_out: bfloat16 [2560, 5120], P('tp'), may hold values from -0.25 to 0.25
- attn_gain: float32 [5120], replicated, may hold values from 0.25 to 1.75
- final_norm_gain: float32 [5120], replicated, may hold values from 0.25 to 1.75
- head_weight: bfloat16 [5120, 76032], P(None, ('req', 'tp')), may hold values from -0.25 to 0.25
- kv_pool: bfloat16 [851968, 4, 256], P('req', 'tp'), may hold values from -17 to 17
- cache_len: int32 [512], replicated, may hold values from 256 to 3072, as said below
Outputs:
- states: bfloat16 [12288, 5120], P('req', 'tp')
- new_kv: bfloat16 [12288, 4, 256], P('req', 'tp')
- row_norms: float32 [512], P('req')
- logit_max: float32 [512], replicated
- logits: float32 [512, 76032], P(None, ('req', 'tp'))
The draws below stay inside these ranges and needn't reach their ends.
Inputs may be any that keep to these rules, and one draw needn't show every extreme that they name: `cache_len`: every cache holds 256 or 3072 rows. Exactly 64 requests hold 3072; requests i * 16 to i * 16 + 15 hold at most 8 of them for every i, and exactly 8 for some i, so their caches fill at most 26624 rows, and exactly 26624 for some i.
All inputs are finite; a program needn't handle non-finite values.
Results may differ from the reference program's by a relative error of at most 0.014.
Values may be sent and summed in bfloat16 or wider, within the bound.
A program may use at most 192 MiB of HBM per device.

```python
import math
import jax
import jax.numpy as jnp
from jax import lax

D = 5120
HD = 128
KVH = 4
GROUP = 5
VOCAB = 76032
NEW = 24
SHORT = 256
LONG = 3072
REQ_DEV = 16
HEADS = 20
LMAX = 8
POOL = 26624
REQUESTS = 512
LONGS = 64
TOKENS = 12288
N_REQ = 32


def draw_tokens(key, part):
    token_count = REQUESTS * NEW
    columns = jnp.arange(D, dtype=jnp.float32)
    rising = 0.75 * jnp.exp(0.5 * math.log(3.0) / (D - 1) * columns)
    base = jnp.clip(jax.random.normal(key, (token_count, D), jnp.float32), -5.0, 5.0)
    return (base * rising[None, :]).astype(jnp.bfloat16)


def draw_query_bias(key, part):
    return jnp.clip(0.5 * jax.random.normal(key, (KVH * GROUP * HD,), jnp.float32), -2.0, 2.0)


def draw_kv_pool(key, part):
    total_rows = N_REQ * POOL
    return jnp.clip(jax.random.normal(key, (total_rows, KVH, 2 * HD), jnp.float32), -4.0, 4.0).astype(jnp.bfloat16)


def draw_cache_len(key, part):
    heavy = max(1, LONGS // (2 * LMAX))
    spare = N_REQ - heavy
    leftover = LONGS - heavy * LMAX
    device_order = jax.random.permutation(jax.random.fold_in(key, 11), N_REQ)
    device_rank = jnp.argsort(device_order).astype(jnp.int32)
    spread_count = (leftover + device_rank - heavy) // spare
    counts = jnp.where(device_rank < heavy, LMAX, spread_count).astype(jnp.int32)
    raw_scores = jax.random.randint(jax.random.fold_in(key, 12), (N_REQ, REQ_DEV), 0, 1 << 20, jnp.int32)
    slot_scores = raw_scores * REQ_DEV + jnp.arange(REQ_DEV, dtype=jnp.int32)[None, :]
    slot_order = jnp.argsort(slot_scores, axis=1)
    slot_rank = jnp.argsort(slot_order, axis=1).astype(jnp.int32)
    lengths = jnp.where(slot_rank < counts[:, None], LONG, SHORT)
    return lengths.reshape(-1).astype(jnp.int32)


def levels(key, shape, split, least, high):
    def one(dim, parts):
        heights = jax.random.uniform(jax.random.fold_in(jax.random.fold_in(key, 6), dim), (parts,), jnp.float32, least / len(split), high / len(split))
        return jnp.repeat(jnp.exp(heights), shape[dim] // parts).reshape((-1,) + (1,) * (len(shape) - dim - 1))

    gain = one(*split[0])
    for cut in split[1:]:
        gain = gain * one(*cut)
    return gain


def bell_draw(key, shape, width, reach, shards=(), kind=jnp.bfloat16):
    values = width * jax.random.normal(key, shape, jnp.float32)
    if shards:
        values = values * levels(key, shape, shards, -0.22, 0.18)
    return jnp.clip(values, -reach, reach).astype(kind)


def setup_inputs(seed: int = 0) -> dict:
    key_of = jax.random.split(jax.random.key(seed), 12)
    return {
        "tokens": draw_tokens(jax.random.fold_in(key_of[11], 71), 0),
        "w_query": bell_draw(key_of[1], (D, HEADS * HD), (D // 2) ** -0.5, 0.125, ((1, 4),)),
        "query_bias": draw_query_bias(jax.random.fold_in(key_of[11], 71), 0),
        "w_keyval": bell_draw(key_of[3], (D, 2 * KVH * HD), (D // 6) ** -0.5, 0.21875, ((1, 4),)),
        "keyval_bias": bell_draw(key_of[4], (2 * KVH * HD,), 0.5, 2.5, ((0, 4),), jnp.float32),
        "w_out": bell_draw(key_of[5], (HEADS * HD, D), (HEADS * HD // 4) ** -0.5, 0.25, ((0, 4),)),
        "attn_gain": jnp.clip(1.0 + 0.15 * jax.random.normal(key_of[6], (D,), jnp.float32), 0.25, 1.75),
        "final_norm_gain": jnp.clip(1.0 + 0.15 * jax.random.normal(key_of[7], (D,), jnp.float32), 0.25, 1.75),
        "head_weight": bell_draw(key_of[8], (D, VOCAB), (D // 9) ** -0.5, 0.25, ((1, 128),)),
        "kv_pool": draw_kv_pool(jax.random.fold_in(key_of[11], 71), 0),
        "cache_len": draw_cache_len(jax.random.fold_in(key_of[11], 71), 0),
    }


THETA = 1000000.0
EPS = 1e-06

def rope_rotate(vectors, positions):
    head_width = vectors.shape[-1]
    halfway = head_width // 2
    frequency = THETA ** (-(jnp.arange(halfway, dtype=jnp.float32) * (2.0 / head_width)))
    angles = positions[..., None] * frequency
    cosine = jnp.cos(angles)
    sine_part = jnp.sin(angles)
    front_part = vectors[..., :halfway]
    back_part = vectors[..., halfway:]
    return jnp.concatenate([front_part * cosine - back_part * sine_part, back_part * cosine + front_part * sine_part], axis=-1)

def attend_one(q_req, k_req, v_req, row_begin, length, kv_pool):
    total_rows = kv_pool.shape[0]
    row_first = jnp.minimum(row_begin, total_rows - LONG).astype(jnp.int32)
    window = lax.dynamic_slice_in_dim(kv_pool, row_first, LONG, 0)
    row_index = row_first + jnp.arange(LONG, dtype=jnp.int32)
    inside = (row_index >= row_begin) & (row_index < row_begin + length)
    query_f = q_req.astype(jnp.float32)
    cache_scores = jnp.einsum('nkgd,lkd->kgnl', query_f, window[..., :HD].astype(jnp.float32))
    cache_scores = jnp.where(inside[None, None, None, :], cache_scores, -jnp.inf)
    new_scores = jnp.einsum('nkgd,mkd->kgnm', query_f, k_req.astype(jnp.float32))
    causal = jnp.arange(NEW, dtype=jnp.int32)[:, None] >= jnp.arange(NEW, dtype=jnp.int32)[None, :]
    new_scores = jnp.where(causal[None, None], new_scores, -jnp.inf)
    scores = jnp.concatenate([cache_scores, new_scores], axis=-1)
    row_max = lax.optimization_barrier(jnp.max(scores, axis=-1, keepdims=True))
    exps = jnp.exp(scores - row_max)
    totals = lax.optimization_barrier(jnp.sum(exps, axis=-1))
    rounded = lax.optimization_barrier(exps.astype(jnp.bfloat16)).astype(jnp.float32)
    value_matrix = jnp.concatenate([window[..., HD:], v_req], axis=0).astype(jnp.float32)
    mixed = jnp.einsum('kgnl,lkd->nkgd', rounded, value_matrix)
    return (mixed / jnp.transpose(totals, (2, 0, 1))[..., None]).astype(jnp.bfloat16)

def reference(tokens, w_query, query_bias, w_keyval, keyval_bias, w_out, attn_gain, final_norm_gain, head_weight, kv_pool, cache_len):
    source = tokens.astype(jnp.float32)
    mean_square = lax.optimization_barrier(jnp.mean(source * source, axis=1, keepdims=True))
    normed = (source / jnp.sqrt(mean_square + EPS) * attn_gain[None, :]).astype(jnp.bfloat16)
    query_raw = jnp.dot(normed, w_query, preferred_element_type=jnp.float32) + query_bias[None, :]
    keyval_raw = jnp.dot(normed, w_keyval, preferred_element_type=jnp.float32) + keyval_bias[None, :]
    positions = (cache_len[:, None] + jnp.arange(NEW, dtype=jnp.int32)[None, :]).astype(jnp.float32)
    query_heads = query_raw.reshape(REQUESTS, NEW, KVH, GROUP, HD)
    queries = (rope_rotate(query_heads, positions[:, :, None, None]) * (1.0 / math.sqrt(HD))).astype(jnp.bfloat16)
    keyval_heads = keyval_raw.reshape(REQUESTS, NEW, KVH, 2, HD)
    key_new = rope_rotate(keyval_heads[:, :, :, 0, :], positions[:, :, None]).astype(jnp.bfloat16)
    value_new = keyval_heads[:, :, :, 1, :].astype(jnp.bfloat16)
    new_kv = jnp.concatenate([key_new, value_new], axis=-1).reshape(TOKENS, KVH, 2 * HD)
    lens_grid = cache_len.reshape(N_REQ, REQ_DEV)
    row_starts = (jnp.arange(N_REQ, dtype=jnp.int32)[:, None] * POOL + jnp.cumsum(lens_grid, axis=1) - lens_grid).reshape(-1).astype(jnp.int32)

    def one_request(inputs):
        q_req, k_req, v_req, row_begin, length = inputs
        return attend_one(q_req, k_req, v_req, row_begin, length, kv_pool)
    mixed = lax.map(one_request, (queries, key_new, value_new, row_starts, cache_len.astype(jnp.int32)))
    attention = mixed.reshape(TOKENS, HEADS * HD)
    projected = jnp.dot(attention, w_out, preferred_element_type=jnp.float32)
    states = (source + projected).astype(jnp.bfloat16)
    last_rows = states.reshape(REQUESTS, NEW, D)[:, NEW - 1, :].astype(jnp.float32)
    row_norms = jnp.sqrt(lax.optimization_barrier(jnp.mean(last_rows * last_rows, axis=1)) + EPS)
    final_rows = (last_rows / row_norms[:, None] * final_norm_gain[None, :]).astype(jnp.bfloat16)
    logits = jnp.dot(final_rows, head_weight, preferred_element_type=jnp.float32)
    logit_max = lax.optimization_barrier(jnp.max(logits, axis=1))
    return (states, new_kv, row_norms, logit_max, logits)
```

```python
import math

import jax
import jax.numpy as jnp
from jax import lax
from jax.experimental import pallas as pl
from jax.experimental.pallas import tpu as pltpu
from jax.sharding import PartitionSpec as P

HD = 128
GROUP = 5
NEW = 24
SHORT = 256
LONG = 3072


THETA = 1000000.0
EPS = 1e-06


def attention_kernel(
    starts_ref, lens_ref, query_ref, keyval_ref, cos_ref, sin_ref, pool_ref, out_ref, new_ref, cache, sems
):
    requests = query_ref.shape[0]

    def fetch(r, rows):
        begin = pl.multiple_of(starts_ref[r], SHORT)
        window = pl.ds(begin, rows)
        return pltpu.make_async_copy(pool_ref.at[window], cache.at[window], sems.at[r])

    def start_copy(r, carry):
        @pl.when(lens_ref[r] == LONG)
        def _():
            fetch(r, LONG).start()

        @pl.when(lens_ref[r] != LONG)
        def _():
            fetch(r, SHORT).start()

        return carry

    lax.fori_loop(0, requests, start_copy, 0)

    def attend(r, rows):
        cosine = cos_ref[r]
        sine = sin_ref[r]

        def rotate(v):
            return v * cosine + pltpu.roll(v, HD // 2, 1) * sine

        heads = [
            rotate(query_ref[r, :, g * HD : (g + 1) * HD]) * (1.0 / math.sqrt(HD))
            for g in range(GROUP)
        ]
        queries = jnp.concatenate(heads, axis=0).astype(jnp.bfloat16)
        key_new = rotate(keyval_ref[r, :, :HD])
        value_new = keyval_ref[r, :, HD:]
        new_ref[r, :, :HD] = key_new
        new_ref[r, :, HD:] = value_new
        pad = jnp.zeros((HD - NEW, HD), jnp.float32)
        key_pad = jnp.concatenate([key_new, pad], axis=0).astype(jnp.bfloat16)
        value_pad = jnp.concatenate([value_new, pad], axis=0).astype(jnp.bfloat16)
        contract = (((1,), (1,)), ((), ()))
        new_scores = lax.dot_general(queries, key_pad, contract, preferred_element_type=jnp.float32)
        token = jnp.concatenate(
            [lax.broadcasted_iota(jnp.int32, (NEW, HD), 0)] * GROUP, axis=0
        )
        column = lax.broadcasted_iota(jnp.int32, (GROUP * NEW, HD), 1)
        new_scores = jnp.where(column <= token, new_scores, -jnp.inf)
        fetch(r, rows).wait()
        window = pl.ds(pl.multiple_of(starts_ref[r], SHORT), rows)
        scores = lax.dot_general(
            queries, cache[window, :HD], contract, preferred_element_type=jnp.float32
        )
        row_max = jnp.maximum(
            jnp.max(scores, axis=1, keepdims=True), jnp.max(new_scores, axis=1, keepdims=True)
        )
        exps = jnp.exp(scores - row_max)
        new_exps = jnp.exp(new_scores - row_max)
        totals = jnp.sum(exps, axis=1, keepdims=True) + jnp.sum(new_exps, axis=1, keepdims=True)
        mixed = jnp.dot(
            exps.astype(jnp.bfloat16), cache[window, HD:], preferred_element_type=jnp.float32
        ) + jnp.dot(new_exps.astype(jnp.bfloat16), value_pad, preferred_element_type=jnp.float32)
        result = mixed / totals
        for g in range(GROUP):
            out_ref[r, :, g * HD : (g + 1) * HD] = result[g * NEW : (g + 1) * NEW, :]

    def step(r, carry):
        @pl.when(lens_ref[r] == LONG)
        def _():
            attend(r, LONG)

        @pl.when(lens_ref[r] != LONG)
        def _():
            attend(r, SHORT)

        return carry

    lax.fori_loop(0, requests, step, 0)


def attend_all(starts, lens, query_raw, keyval_raw, cosine, sine, pool):
    requests = lens.shape[0]
    smem = pl.BlockSpec(memory_space=pltpu.SMEM)
    vmem = pl.BlockSpec(memory_space=pltpu.VMEM)
    return pl.pallas_call(
        attention_kernel,
        out_shape=(
            jax.ShapeDtypeStruct(query_raw.shape, jnp.float32),
            jax.ShapeDtypeStruct(keyval_raw.shape, jnp.float32),
        ),
        in_specs=[smem, smem, vmem, vmem, vmem, vmem, pl.BlockSpec(memory_space=pl.ANY)],
        out_specs=(vmem, vmem),
        scratch_shapes=[
            pltpu.VMEM(pool.shape, pool.dtype),
            pltpu.SemaphoreType.DMA((requests,)),
        ],
        compiler_params=pltpu.CompilerParams(vmem_limit_bytes=48 * 1024 * 1024),
    )(starts, lens, query_raw, keyval_raw, cosine, sine, pool)


def local(
    tokens,
    w_query,
    query_bias,
    w_keyval,
    keyval_bias,
    w_out,
    attn_gain,
    final_norm_gain,
    head_weight,
    kv_pool,
    cache_len,
):
    groups = lax.axis_size("req")
    my_group = lax.axis_index("req")
    tp_count = lax.axis_size("tp")
    tp_index = lax.axis_index("tp")
    tok_rows = tokens.shape[0]
    model_width = tokens.shape[1]
    per_group = tok_rows // NEW
    kv_local = kv_pool.shape[1]
    lens_grid = cache_len.reshape(groups, per_group)
    my_lens = lax.dynamic_slice_in_dim(lens_grid, my_group, 1, 0)[0]
    my_starts = jnp.cumsum(my_lens) - my_lens
    source = tokens.astype(jnp.float32)
    mean_square = jnp.mean(source * source, axis=1, keepdims=True)
    normed = (source / jnp.sqrt(mean_square + EPS) * attn_gain[None, :]).astype(jnp.bfloat16)
    query_raw = jnp.dot(normed, w_query, preferred_element_type=jnp.float32) + query_bias[None, :]
    keyval_raw = (
        jnp.dot(normed, w_keyval, preferred_element_type=jnp.float32) + keyval_bias[None, :]
    )
    positions = (my_lens[:, None] + jnp.arange(NEW, dtype=jnp.int32)[None, :]).astype(jnp.float32)
    half = HD // 2
    frequency = THETA ** (-(jnp.arange(half, dtype=jnp.float32) * (2.0 / HD)))
    angles = positions[..., None] * frequency
    cosine = jnp.cos(angles)
    sine = jnp.sin(angles)
    mixed, new_rows = attend_all(
        my_starts.astype(jnp.int32),
        my_lens.astype(jnp.int32),
        query_raw.reshape(per_group, NEW, GROUP * HD),
        keyval_raw.reshape(per_group, NEW, 2 * HD),
        jnp.concatenate([cosine, cosine], axis=-1),
        jnp.concatenate([-sine, sine], axis=-1),
        kv_pool.reshape(kv_pool.shape[0], 2 * HD),
    )
    new_kv = new_rows.astype(jnp.bfloat16).reshape(tok_rows, kv_local, 2 * HD)
    attention = mixed.astype(jnp.bfloat16).reshape(tok_rows, GROUP * HD)
    partial_value = jnp.dot(attention, w_out, preferred_element_type=jnp.float32)
    width_local = model_width // tp_count
    summed = lax.psum_scatter(
        partial_value.astype(jnp.bfloat16), "tp", scatter_dimension=1, tiled=True
    ).astype(jnp.float32)
    source_part = lax.dynamic_slice_in_dim(tokens, tp_index * width_local, width_local, 1)
    states = (source_part.astype(jnp.float32) + summed).astype(jnp.bfloat16)
    last_part = states.reshape(per_group, NEW, width_local)[:, NEW - 1, :]
    gathered = lax.all_gather(last_part, ("req", "tp"), axis=0, tiled=False)
    last_rows = (
        jnp.transpose(gathered.reshape(groups, tp_count, per_group, width_local), (0, 2, 1, 3))
        .reshape(groups * per_group, model_width)
        .astype(jnp.float32)
    )
    all_norms = jnp.sqrt(jnp.mean(last_rows * last_rows, axis=1) + EPS)
    row_norms = lax.dynamic_slice_in_dim(all_norms, my_group * per_group, per_group, 0)
    final_rows = (last_rows / all_norms[:, None] * final_norm_gain[None, :]).astype(jnp.bfloat16)
    logits = jnp.dot(final_rows, head_weight, preferred_element_type=jnp.float32)
    local_max = jnp.max(logits, axis=1)
    logit_max = jnp.max(lax.all_gather(local_max, ("req", "tp"), axis=0, tiled=False), axis=0)
    return (states, new_kv, row_norms, logit_max, logits)


def solution(mesh):
    return jax.shard_map(
        local,
        mesh=mesh,
        in_specs=(
            P("req", None),
            P(None, "tp"),
            P("tp"),
            P(None, "tp"),
            P("tp"),
            P("tp", None),
            P(),
            P(),
            P(None, ("req", "tp")),
            P("req", "tp", None),
            P(),
        ),
        out_specs=(P("req", "tp"), P("req", "tp", None), P("req"), P(), P(None, ("req", "tp"))),
        check_vma=False,
    )
```
